1024 devices in a mesh: band: 64 (over x, z), mem: 16 (over y, core).
Axes of the slice: x: 4, y: 8, z: 16, core: 2. Of those that a mesh axis runs over, the one named last changes fastest.
Arguments:
- state: float32 [1024, 512, 256], P('mem', 'band'), may hold values from -6 to 6
- courant: float32 [2, 512, 256], P(None, 'band'), may hold values from 0.15 to 0.4
- obs_pert: bfloat16 [64, 512, 1024], P('band'), may hold values from -8 to 8
- obs_cell: int32 [64, 512], P('band'), may hold values from 0 to 131071, as said below
- block_rows: int32 [64], replicated, may hold values from 64 to 512, as said below
- band_list: int32 [64, 2], P('band'), may hold values from 0 to 63, as said below
Outputs:
- analysis: float32 [1024, 512, 256], P('mem', 'band')
The draws below stay inside these ranges and needn't reach their ends.
Inputs may be any that keep to these rules, and one draw needn't show every extreme that they name: `band_list`: row b holds 2 different block numbers, each one of b - 1, b, b + 1 taken modulo 64. `block_rows`: the first that many rows of a block are live. Some block has exactly 512 in every draw. `obs_cell`: the rows of block j lie in latitude rows j * 8 to (j + 1) * 8 - 1; a cell is numbered latitude row times 256 plus longitude.
All inputs are finite; a program needn't handle non-finite values.
Results may differ from the reference program's by a relative error of at most 0.0045.
Values may be sent and summed in bfloat16 or wider, within the bound.
No kernel may reach another device: no remote copies, remote signals or barrier semaphores. Data moves between devices by JAX's collectives and lax.ppermute only.
A program may use at most 32 MiB of HBM per device.

```python
import jax
import jax.numpy as jnp
from jax import lax

MEMBERS = 1024
ROWS_BAND = 8
LON = 256
STEPS = 6
OBS_ROWS = 512
LIST = 2
DEGREE = 4
BLOCKS = 64
NLAT = 512
N_BAND = 64


def draw_band_list(key, part):
    scores = jax.random.randint(key, (BLOCKS, 3), 0, 1 << 20) * 4 + jnp.arange(3, dtype=jnp.int32)[None, :]
    chosen = jnp.argsort(scores, axis=1, stable=True)[:, :LIST].astype(jnp.int32)
    listed = (jnp.arange(BLOCKS, dtype=jnp.int32)[:, None] + chosen - 1) % BLOCKS
    return listed.astype(jnp.int32)


def draw_block_rows(key, part):
    first_key, second_key = jax.random.split(key)
    counts = jax.random.randint(first_key, (BLOCKS,), OBS_ROWS // 8, OBS_ROWS + 1)
    fullest = jax.random.randint(second_key, (), 0, BLOCKS)
    counts = jnp.where(jnp.arange(BLOCKS, dtype=jnp.int32) == fullest, OBS_ROWS, counts)
    return counts.astype(jnp.int32)


def draw_obs_cell(key, part):
    inside = jax.random.randint(key, (BLOCKS, OBS_ROWS), 0, ROWS_BAND * LON)
    offsets = jnp.arange(BLOCKS, dtype=jnp.int32)[:, None] * (ROWS_BAND * LON)
    return (inside + offsets).astype(jnp.int32)


def steps_of(rng, dims, shards, smallest, largest):
    def one(axis_at, blocks):
        heights = jax.random.uniform(jax.random.fold_in(jax.random.fold_in(rng, 6), axis_at), (blocks,), jnp.float32, smallest / len(shards), largest / len(shards))
        return jnp.repeat(jnp.exp(heights), dims[axis_at] // blocks).reshape((-1,) + (1,) * (len(dims) - axis_at - 1))

    level = one(*shards[0])
    for cut in shards[1:]:
        level = level * one(*cut)
    return level


def normal_values(own_key, shape, deviation, bound, cuts=(), kind=jnp.bfloat16):
    level = steps_of(own_key, shape, cuts, -0.22, 0.18) if cuts else 1.0
    result = jax.random.normal(own_key, shape, jnp.float32) * deviation * level
    return jnp.minimum(jnp.maximum(result, -bound), bound).astype(kind)


def setup_inputs(seed: int = 0) -> dict:
    splits = jax.random.split(jax.random.key(seed), 7)
    return {
        "state": normal_values(splits[0], (MEMBERS, NLAT, LON), 1.0, 6.0, ((0, 16), (1, 64)), jnp.float32),
        "courant": jnp.clip(0.15 + 0.25 * jax.random.uniform(splits[1], (2, NLAT, LON), jnp.float32) ** steps_of(splits[1], (2, NLAT, LON), ((1, 64),), -0.2, 0.2), 0.15, 0.4),
        "obs_pert": normal_values(splits[2], (BLOCKS, OBS_ROWS, MEMBERS), 1.8, 8.0, ((0, 64),)),
        "obs_cell": draw_obs_cell(jax.random.fold_in(splits[6], 71), 0),
        "block_rows": draw_block_rows(jax.random.fold_in(splits[6], 71), 0),
        "band_list": draw_band_list(jax.random.fold_in(splits[6], 71), 0),
    }


DIFFUSION = 0.05
COEFFS = (1.0, -0.5, 0.375, -0.3125, 0.2734375)


def advance_member(tracer, courant):
    northern = jnp.roll(tracer, 1, axis=0)
    southern = jnp.roll(tracer, -1, axis=0)
    western = jnp.roll(tracer, 1, axis=1)
    eastern = jnp.roll(tracer, -1, axis=1)
    saturation = 0.5 + 0.5 * jnp.tanh(tracer)
    return (tracer - courant[0] * saturation * (tracer - northern)
            - courant[1] * saturation * (tracer - western)
            + DIFFUSION * (northern + southern + eastern + western - 4.0 * tracer))


def localization(obs_cells, live_rows, cell_flat, lat_count, lon_count, rows_band, gscale):
    obs_lat = obs_cells // lon_count
    obs_lon = obs_cells % lon_count
    cell_lat = cell_flat // lon_count
    cell_lon = cell_flat % lon_count
    lat_gap = jnp.abs(obs_lat[:, None] - cell_lat[None, :])
    lat_gap = jnp.minimum(lat_gap, lat_count - lat_gap)
    lon_gap = jnp.abs(obs_lon[:, None] - cell_lon[None, :])
    lon_gap = jnp.minimum(lon_gap, lon_count - lon_gap)
    lat_term = lat_gap.astype(jnp.float32) * (1.0 / rows_band)
    lon_term = lon_gap.astype(jnp.float32) * (4.0 / lon_count)
    decay = jnp.exp(-0.5 * (lat_term * lat_term + lon_term * lon_term)) * gscale
    return jnp.where(live_rows[:, None], decay, jnp.zeros_like(decay))


def transform(pert, observed, weight):
    series = pert
    combined = COEFFS[0] * pert
    for power in range(1, DEGREE + 1):
        projected = jnp.dot(observed, series.astype(jnp.bfloat16), preferred_element_type=jnp.float32)
        scaled = (projected * weight).astype(jnp.bfloat16)
        series = lax.dot_general(observed, scaled, (((0,), (0,)), ((), ())), preferred_element_type=jnp.float32)
        combined = combined + COEFFS[power] * series
    return combined


def reference(state, courant, obs_pert, obs_cell, block_rows, band_list):
    def run_member(tracer):
        for section in range(STEPS):
            tracer = advance_member(tracer, courant)
        return tracer

    advected = lax.map(run_member, state)
    band_cells = ROWS_BAND * LON
    gscale = 1.0 / (MEMBERS + LIST * OBS_ROWS)

    def per_band(band_index):
        columns = lax.dynamic_slice_in_dim(advected, band_index * ROWS_BAND, ROWS_BAND, 1)
        columns = columns.reshape(MEMBERS, band_cells)
        average = jnp.mean(columns, axis=0, keepdims=True)
        pert = columns - average
        block_ids = band_list[band_index]
        observed = obs_pert[block_ids].reshape(LIST * OBS_ROWS, MEMBERS)
        obs_cells = obs_cell[block_ids].reshape(LIST * OBS_ROWS)
        live_rows = (jnp.arange(OBS_ROWS, dtype=jnp.int32)[None, :] < block_rows[block_ids][:, None]).reshape(-1)
        cell_flat = band_index * band_cells + jnp.arange(band_cells, dtype=jnp.int32)
        weight = localization(obs_cells, live_rows, cell_flat, NLAT, LON, ROWS_BAND, gscale)
        return average + transform(pert, observed, weight)

    analysed = lax.map(per_band, jnp.arange(N_BAND, dtype=jnp.int32))
    analysed = analysed.reshape(N_BAND, MEMBERS, ROWS_BAND, LON).transpose(1, 0, 2, 3)
    return analysed.reshape(MEMBERS, NLAT, LON)
```

```python
import functools

import jax
import jax.numpy as jnp
from jax import lax
from jax.experimental import pallas as pl
from jax.experimental.pallas import tpu as pltpu
from jax.sharding import PartitionSpec as P


STEPS = 6
LIST = 2
DEGREE = 4

DIFFUSION = 0.05
COEFFS = (1.0, -0.5, 0.375, -0.3125, 0.2734375)

F32 = jnp.float32
BF16 = jnp.bfloat16
VMEM = pl.BlockSpec(memory_space=pltpu.VMEM)
PARAMS = pltpu.CompilerParams(vmem_limit_bytes=16 << 20)
SMEM = pl.BlockSpec(memory_space=pltpu.SMEM)
ANY = pl.BlockSpec(memory_space=pl.ANY)

EXTRA = 8
LANES = 128


def in_vmem(x):
    return pltpu.with_memory_space_constraint(x, pltpu.VMEM)


def pack(members, rows, state_ref, courant_ref, cells_ref, towards_a_ref, towards_b_ref, fields_ref):
    even = lax.rem(lax.axis_index("band"), 2) == 0
    lon = fields_ref.shape[2]
    sides = lon // LANES
    for row in range(rows):
        for side in range(sides):
            fields_ref[row, :, side * LANES : (side + 1) * LANES] = state_ref[
                pl.ds(side * rows + row, members, stride=sides * rows), :
            ]
    place = lax.broadcasted_iota(jnp.int32, (EXTRA, lon), 0)
    cells = cells_ref[...]
    lat = jnp.bitwise_and(lax.shift_right_logical(cells, 8), rows - 1).astype(F32)
    east = jnp.bitwise_and(cells, lon - 1).astype(F32)
    obs = jnp.zeros((EXTRA, lon), F32)
    for slot, values in ((4, lat[:, :lon]), (5, lat[:, lon:]), (6, east[:, :lon]), (7, east[:, lon:])):
        obs = jnp.where(place == slot, values, obs)
    for message_ref, from_tail in ((towards_a_ref, even), (towards_b_ref, jnp.logical_not(even))):
        first = jnp.where(from_tail, rows - STEPS, 0)
        for step in range(STEPS):
            message_ref[step, :members, :] = fields_ref[first + step].astype(BF16)
            extra = obs
            for wind in range(2):
                value = jnp.where(
                    from_tail,
                    courant_ref[wind, rows - STEPS + step : rows - STEPS + step + 1, :],
                    courant_ref[wind, step : step + 1, :],
                )
                high = value.astype(BF16).astype(F32)
                extra = jnp.where(place == wind, high, extra)
                extra = jnp.where(place == wind + 2, value - high, extra)
            message_ref[step, members:, :] = extra.astype(BF16)


def advect(members, rows, fields_ref, courant_ref, from_a_ref, from_b_ref, groups_ref, near_ref, held, winds):
    even = lax.rem(lax.axis_index("band"), 2) == 0
    lon = fields_ref.shape[2]
    total = rows + 2 * STEPS

    extra_a = from_a_ref[0, members:, :].astype(F32)
    extra_b = from_b_ref[0, members:, :].astype(F32)
    near_ref[0] = jnp.where(even, extra_b, extra_a)
    near_ref[1] = jnp.where(even, extra_a, extra_b)

    def keep(row, value0, value1):
        for wind, value in ((0, value0), (1, value1)):
            half = 0.5 * jnp.broadcast_to(value, (8, lon))
            winds[row, 2 * wind] = half
            winds[row, 2 * wind + 1] = half + DIFFUSION

    for message_ref, first in (
        (from_a_ref, jnp.where(even, STEPS + rows, 0)),
        (from_b_ref, jnp.where(even, 0, STEPS + rows)),
    ):
        for step in range(STEPS):
            held[first + step] = message_ref[step, :members, :].astype(F32)
            extra = message_ref[step, members:, :].astype(F32)
            keep(first + step, extra[0:1] + extra[2:3], extra[1:2] + extra[3:4])
    for row in range(rows):
        keep(STEPS + row, courant_ref[0, row : row + 1, :], courant_ref[1, row : row + 1, :])

    lane = lax.broadcasted_iota(jnp.int32, (8, LANES), 1)
    sides = lon // LANES

    def turned(parts, shift, edge):
        way = -1 if shift == 1 else 1
        mixed = [jnp.where(lane == edge, parts[(side + way) % sides], parts[side]) for side in range(sides)]
        return [pltpu.roll(part, shift % LANES, 1) for part in mixed]

    def group(index, carry):
        first = pl.multiple_of(index * 8, 8)

        def read(ref, row):
            return [ref[row, pl.ds(first, 8), side * LANES : (side + 1) * LANES] for side in range(sides)]

        def minus(left, right):
            return [x - y for x, y in zip(left, right)]

        values = [
            read(fields_ref, row - STEPS) if STEPS <= row < STEPS + rows else read(held, row) for row in range(total)
        ]
        for step in range(1, STEPS + 1):
            fresh = list(values)
            north = minus(values[step], values[step - 1])
            for row in range(step, total - step):
                centre = values[row]
                south = minus(values[row + 1], centre)
                west = minus(centre, turned(centre, 1, LANES - 1))
                east = turned(west, -1, 0)
                new = []
                for side in range(sides):
                    lanes = slice(side * LANES, (side + 1) * LANES)
                    curve = jnp.tanh(centre[side])
                    new.append(
                        centre[side]
                        - north[side] * (winds[row, 0, :, lanes] * curve + winds[row, 1, :, lanes])
                        - west[side] * (winds[row, 2, :, lanes] * curve + winds[row, 3, :, lanes])
                        + DIFFUSION * (south[side] + east[side])
                    )
                fresh[row] = new
                north = south
            values = fresh
        for row in range(rows):
            for side in range(sides):
                held[row, pl.ds(first, 8), side * LANES : (side + 1) * LANES] = values[STEPS + row][side]
        return carry

    lax.fori_loop(0, members // 8, group, 0)
    for row in range(rows):
        groups_ref[2 * row] = held[row, :, : lon // 2].astype(BF16)
        groups_ref[2 * row + 1] = held[row, :, lon // 2 :].astype(BF16)


def place_of(listed_ref, position):
    band, bands = lax.axis_index("band"), lax.axis_size("band")
    return lax.rem(listed_ref[0, position] - band + 1 + bands, bands)


def localize(rows, lon, gscale, listed_ref, counts_ref, cells_ref, near_ref, weight_ref):
    mem = lax.axis_index("mem")
    group_cells, obs_total = weight_ref.shape
    obs_rows = obs_total // LIST
    cells = cells_ref[...]
    own_lat = jnp.bitwise_and(lax.shift_right_logical(cells, 8), rows - 1).astype(F32)
    own_lon = jnp.bitwise_and(cells, lon - 1).astype(F32)

    def pair(side, slot):
        return jnp.concatenate([near_ref[side, slot : slot + 1, :], near_ref[side, slot + 1 : slot + 2, :]], axis=1)

    halves = lon // group_cells
    cell_row = (mem // halves).astype(F32)
    cell_lon = (
        lax.broadcasted_iota(jnp.int32, (group_cells, obs_rows), 0) + lax.rem(mem, halves) * group_cells
    ).astype(F32)
    lane = lax.broadcasted_iota(jnp.int32, (group_cells, obs_rows), 1)
    for position in range(LIST):
        place = place_of(listed_ref, position)
        lat = jnp.where(place == 0, pair(0, 4), jnp.where(place == 1, own_lat, pair(1, 4)))
        east = jnp.where(place == 0, pair(0, 6), jnp.where(place == 1, own_lon, pair(1, 6)))
        lat_gap = jnp.abs(lat + (place - 1).astype(F32) * rows - cell_row) * (1.0 / rows)
        lon_gap = jnp.abs(jnp.broadcast_to(east, cell_lon.shape) - cell_lon)
        lon_gap = jnp.minimum(lon_gap, lon - lon_gap) * (4.0 / lon)
        decay = jnp.exp(-0.5 * (jnp.broadcast_to(lat_gap * lat_gap, lon_gap.shape) + lon_gap * lon_gap)) * gscale
        live = lane < counts_ref[listed_ref[0, position]]
        weight_ref[:, position * obs_rows : (position + 1) * obs_rows] = jnp.where(live, decay, 0.0)


def transform(
    listed_ref, columns_ref, weight_hbm, own_ref, fetched_ref, swapped_ref, analysed_ref, observed_ref, weight_ref, sems
):
    shares, share, cells = columns_ref.shape
    obs_rows = own_ref.shape[1]
    first_core = lax.rem(lax.axis_index("mem"), 2) == 0
    copies = []
    for position in range(LIST):
        target = observed_ref.at[pl.ds(position * obs_rows, obs_rows), :]
        place = place_of(listed_ref, position)
        near = place != 1
        fetched = jnp.logical_and(near, (place == 0) == first_core)
        swapped = jnp.logical_and(near, (place == 0) != first_core)
        for chosen, source in ((place == 1, own_ref), (fetched, fetched_ref), (swapped, swapped_ref)):
            copy = pltpu.make_async_copy(source.at[0], target, sems.at[position])
            pl.when(chosen)(copy.start)
        copies.append(copy)
    weight_copy = pltpu.make_async_copy(weight_hbm, weight_ref, sems.at[LIST])
    weight_copy.start()
    columns = jnp.transpose(columns_ref[...].reshape(shares * share, cells)).astype(F32)
    average = jnp.mean(columns, axis=1, keepdims=True)
    series = columns - average
    combined = COEFFS[0] * series
    for copy in copies + [weight_copy]:
        copy.wait()
    for power in range(1, DEGREE + 1):
        projected = lax.dot_general(
            series.astype(BF16), observed_ref[...], (((1,), (1,)), ((), ())), preferred_element_type=F32
        )
        scaled = (projected * weight_ref[...]).astype(BF16)
        series = jnp.dot(scaled, observed_ref[...], preferred_element_type=F32)
        combined = combined + COEFFS[power] * series
    analysed = (average + combined).astype(BF16)
    analysed_ref[...] = jnp.transpose(analysed).reshape(shares, share, cells)


def unpack(members, rows, returned_ref, out_ref):
    for row in range(rows):
        for side in range(2):
            out_ref[pl.ds(side * rows + row, members, stride=2 * rows), :] = returned_ref[2 * row + side].astype(F32)


def shards(state, courant, obs_pert, obs_cell, block_rows, band_list):
    members, rows, lon = state.shape
    bands = lax.axis_size("band")
    shares = lax.axis_size("mem")
    obs_rows, all_members = obs_pert.shape[1:]
    cells = rows * lon // shares
    message = pltpu.VMEM((STEPS, members + EXTRA, lon), BF16)
    towards_a, towards_b, fields = pl.pallas_call(
        functools.partial(pack, members, rows),
        out_shape=(message, message, pltpu.VMEM((rows, members, lon), F32)),
        in_specs=[VMEM] * 3,
        out_specs=(VMEM,) * 3,
        compiler_params=PARAMS,
        name="pack",
    )(state.reshape(members, rows, lon // LANES, LANES).transpose(0, 2, 1, 3).reshape(-1, LANES), courant, obs_cell)
    pairs_a = [(band, band ^ 1) for band in range(bands)]
    pairs_b = [(band, (band + (1 if band % 2 else -1)) % bands) for band in range(bands)]
    from_b = lax.ppermute(towards_b, "band", pairs_b)
    from_a = lax.ppermute(towards_a, "band", pairs_a)
    ring = [
        (band * shares + mem, (band + (-1 if mem % 2 else 1)) % bands * shares + mem)
        for band in range(bands)
        for mem in range(shares)
    ]
    source, _ = lax.optimization_barrier((obs_pert, towards_b))
    fetched = lax.ppermute(source, ("band", "mem"), ring)
    groups, near = pl.pallas_call(
        functools.partial(advect, members, rows),
        out_shape=(
            pltpu.VMEM((shares, members, cells), BF16),
            jax.ShapeDtypeStruct((2, EXTRA, lon), F32),
        ),
        in_specs=[VMEM] * 4,
        out_specs=(VMEM,) * 2,
        scratch_shapes=[
            pltpu.VMEM((rows + 2 * STEPS, members, lon), F32),
            pltpu.VMEM((rows + 2 * STEPS, 4, 8, lon), F32),
        ],
        compiler_params=PARAMS,
        name="advect",
    )(in_vmem(fields), courant, in_vmem(from_a), in_vmem(from_b))
    columns = lax.all_to_all(groups, "mem", split_axis=0, concat_axis=0, tiled=True)
    held, _ = lax.optimization_barrier((fetched, groups))
    swapped = lax.ppermute(held, "mem", [(mem, mem ^ 1) for mem in range(shares)])
    weight = pl.pallas_call(
        functools.partial(localize, rows, lon, 1.0 / (all_members + LIST * obs_rows)),
        out_shape=jax.ShapeDtypeStruct((cells, LIST * obs_rows), F32),
        in_specs=[SMEM, SMEM, VMEM, VMEM],
        out_specs=VMEM,
        compiler_params=PARAMS,
        name="localize",
    )(band_list, block_rows, obs_cell, near)
    analysed = pl.pallas_call(
        transform,
        out_shape=pltpu.VMEM((shares, members, cells), BF16),
        in_specs=[SMEM, VMEM, ANY, ANY, ANY, ANY],
        out_specs=VMEM,
        scratch_shapes=[
            pltpu.VMEM((LIST * obs_rows, all_members), BF16),
            pltpu.VMEM((cells, LIST * obs_rows), F32),
            pltpu.SemaphoreType.DMA((LIST + 1,)),
        ],
        compiler_params=PARAMS,
        name="transform",
    )(band_list, in_vmem(columns), weight, obs_pert, fetched, swapped)
    returned = lax.all_to_all(analysed, "mem", split_axis=0, concat_axis=0, tiled=True)
    out = pl.pallas_call(
        functools.partial(unpack, members, rows),
        out_shape=jax.ShapeDtypeStruct((members * 2 * rows, LANES), F32),
        in_specs=[VMEM],
        out_specs=VMEM,
        compiler_params=pltpu.CompilerParams(vmem_limit_bytes=16 << 20),
        name="unpack",
    )(in_vmem(returned))
    return out.reshape(members, 2, rows, LANES).transpose(0, 2, 1, 3).reshape(members, rows, lon)


def solution(mesh):
    return jax.shard_map(
        shards,
        mesh=mesh,
        in_specs=(
            P("mem", "band", None),
            P(None, "band", None),
            P("band", None, None),
            P("band", None),
            P(),
            P("band", None),
        ),
        out_specs=P("mem", "band", None),
        check_vma=False,
    )
```

```python
import functools

import jax
import jax.numpy as jnp
from jax import lax
from jax.experimental import pallas as pl
from jax.experimental.pallas import tpu as pltpu
from jax.sharding import PartitionSpec as P


STEPS = 6
LIST = 2
DEGREE = 4

DIFFUSION = 0.05
COEFFS = (1.0, -0.5, 0.375, -0.3125, 0.2734375)

F32 = jnp.float32
BF16 = jnp.bfloat16
VMEM = pl.BlockSpec(memory_space=pltpu.VMEM)
PARAMS = pltpu.CompilerParams(vmem_limit_bytes=16 << 20)
SMEM = pl.BlockSpec(memory_space=pltpu.SMEM)
ANY = pl.BlockSpec(memory_space=pl.ANY)
HBM = pl.BlockSpec(memory_space=pltpu.HBM)

EXTRA = 8
SEND_SCALE = 4096.0
LANES = 128
GROUP = 32


def in_vmem(x):
    return pltpu.with_memory_space_constraint(x, pltpu.VMEM)


def in_hbm(x):
    return pltpu.with_memory_space_constraint(x, pltpu.HBM)


def pack(
    members, rows, state_hbm, courant_hbm, cells_hbm, southward_ref, northward_ref, fields_ref, winds_ref,
    state_ref, courant_ref, cells_ref, sems,
):
    copies = [
        pltpu.make_async_copy(source, target, sems.at[slot])
        for slot, (source, target) in enumerate(
            ((state_hbm, state_ref), (courant_hbm, courant_ref), (cells_hbm, cells_ref))
        )
    ]
    for copy in copies:
        copy.start()
    for copy in copies[1:]:
        copy.wait()
    lon = fields_ref.shape[2]
    sides = lon // LANES
    place = lax.broadcasted_iota(jnp.int32, (EXTRA, lon), 0)
    cells = cells_ref[...]
    lat = jnp.bitwise_and(lax.shift_right_logical(cells, 8), rows - 1).astype(F32)
    east = jnp.bitwise_and(cells, lon - 1).astype(F32)
    obs = jnp.zeros((EXTRA, lon), F32)
    for slot, values in ((4, lat[:, :lon]), (5, lat[:, lon:]), (6, east[:, :lon]), (7, east[:, lon:])):
        obs = jnp.where(place == slot, values, obs)
    for message_ref, first in ((southward_ref, rows - STEPS), (northward_ref, 0)):
        for step in range(STEPS):
            extra = obs
            for wind in range(2):
                value = courant_ref[wind, first + step : first + step + 1, :]
                high = value.astype(BF16).astype(F32)
                extra = jnp.where(place == wind, high, extra)
                extra = jnp.where(place == wind + 2, value - high, extra)
            message_ref[step, members:, :] = extra.astype(BF16)
    for row in range(rows):
        keep_winds(winds_ref, row, courant_ref[0, row : row + 1, :], courant_ref[1, row : row + 1, :])
    copies[0].wait()
    for row in range(rows):
        for side in range(sides):
            lanes = slice(side * LANES, (side + 1) * LANES)
            values = state_ref[pl.ds(side * rows + row, members, stride=sides * rows), :]
            fields_ref[row, :, lanes] = values
            if row >= rows - STEPS:
                southward_ref[row - rows + STEPS, :members, lanes] = values.astype(BF16)
            if row < STEPS:
                northward_ref[row, :members, lanes] = values.astype(BF16)


def keep_winds(winds_ref, row, value0, value1):
    for wind, value in ((0, value0), (1, value1)):
        half = 0.5 * jnp.broadcast_to(value, winds_ref.shape[2:])
        winds_ref[row, 2 * wind] = half
        winds_ref[row, 2 * wind + 1] = half + DIFFUSION


def open_message(members, message_ref, halo_ref, winds_ref):
    for step in range(STEPS):
        halo_ref[step] = message_ref[step, :members, :].astype(F32)
        extra = message_ref[step, members:, :].astype(F32)
        keep_winds(winds_ref, step, extra[0:1] + extra[2:3], extra[1:2] + extra[3:4])


def minus(left, right):
    return [x - y for x, y in zip(left, right)]


def turned(parts, way, edge, lane):
    mixed = [jnp.where(lane == edge, parts[(side - way) % len(parts)], part) for side, part in enumerate(parts)]
    return [pltpu.roll(part, way % LANES, 1) for part in mixed]


def march(values, first, last, wind, lane):
    fresh = {}
    north = minus(values[first], values[first - 1])
    for row in range(first, last + 1):
        centre = values[row]
        south = minus(values[row + 1], centre)
        west = minus(centre, turned(centre, 1, LANES - 1, lane))
        east = turned(west, -1, 0, lane)
        new = []
        for side, value in enumerate(centre):
            curve = jnp.tanh(value)
            new.append(
                value
                - north[side] * (wind(row, 0, side) * curve + wind(row, 1, side))
                - west[side] * (wind(row, 2, side) * curve + wind(row, 3, side))
                + DIFFUSION * (south[side] + east[side])
            )
        fresh[row] = new
        north = south
    return fresh


def by_group(members, lon, body):
    lane = lax.broadcasted_iota(jnp.int32, (GROUP, LANES), 1)
    sides = [slice(side * LANES, (side + 1) * LANES) for side in range(lon // LANES)]

    def run(index, carry):
        group = pl.ds(pl.multiple_of(index * GROUP, GROUP), GROUP)

        def read(ref, row):
            return [ref[row, group, lanes] for lanes in sides]

        def write(ref, row, parts):
            for lanes, part in zip(sides, parts):
                ref[row, group, lanes] = part

        body(read, write, lane)
        return carry

    lax.fori_loop(0, members // GROUP, run, 0)


def wind_of(winds_ref, halo_winds_ref=None, halo_first=0):
    def wind(row, kind, side):
        lanes = slice(side * LANES, (side + 1) * LANES)
        if 0 <= row < winds_ref.shape[0]:
            value = winds_ref[row, kind, :, lanes]
        else:
            value = halo_winds_ref[row - halo_first, kind, :, lanes]
        return jnp.concatenate([value] * (GROUP // value.shape[0]), axis=0)

    return wind


INNER = ((1, 1), (1, 2), (1, 5), (1, 6), (2, 2), (2, 3), (2, 4), (2, 5), (3, 3), (3, 4))
UPPER = ((4, 2), (4, 3), (5, 1), (5, 2), (6, 0), (6, 1))


def inner(members, rows, fields_ref, winds_ref, inner_ref):
    def body(read, write, lane):
        values = {row: read(fields_ref, row) for row in range(rows)}
        for step in range(1, rows // 2):
            values = march(values, step, rows - 1 - step, wind_of(winds_ref), lane)
            for slot, (at, row) in enumerate(INNER):
                if at == step:
                    write(inner_ref, slot, values[row])

    by_group(members, fields_ref.shape[2], body)


def upper(members, rows, fields_ref, winds_ref, inner_ref, message_ref, upper_ref, halo_ref, halo_winds_ref):
    open_message(members, message_ref, halo_ref, halo_winds_ref)
    wind = wind_of(winds_ref, halo_winds_ref, -STEPS)

    def body(read, write, lane):
        values = {row - STEPS: read(halo_ref, row) for row in range(STEPS)}
        values.update({row: read(fields_ref, row) for row in range(2)})
        for step in range(1, STEPS + 1):
            values = march(values, step - STEPS, min(step - 1, rows - 1 - step), wind, lane)
            for row in (step, step + 1):
                if (step, row) in INNER:
                    values[row] = read(inner_ref, INNER.index((step, row)))
            for slot, (at, row) in enumerate(UPPER):
                if at == step:
                    write(upper_ref, slot, values[row])

    by_group(members, fields_ref.shape[2], body)


def lower(
    members, rows, fields_ref, winds_ref, inner_ref, upper_ref, above_ref, message_ref, groups_ref, near_ref,
    halo_ref, halo_winds_ref,
):
    near_ref[0] = above_ref[0, members:, :].astype(F32)
    near_ref[1] = message_ref[0, members:, :].astype(F32)
    open_message(members, message_ref, halo_ref, halo_winds_ref)
    wind = wind_of(winds_ref, halo_winds_ref, rows)
    sides = fields_ref.shape[2] // LANES

    def body(read, write, lane):
        values = {rows + row: read(halo_ref, row) for row in range(STEPS)}
        values.update({row: read(fields_ref, row) for row in (rows - 2, rows - 1)})
        for step in range(1, STEPS + 1):
            values = march(values, rows - step, rows + STEPS - 1 - step, wind, lane)
            for row in (rows - 2 - step, rows - 1 - step):
                if (step, row) in INNER:
                    values[row] = read(inner_ref, INNER.index((step, row)))
                elif (step, row) in UPPER:
                    values[row] = read(upper_ref, UPPER.index((step, row)))
        for row in range(rows):
            for side, part in enumerate(values[row]):
                write(groups_ref, sides * row + side, [part * SEND_SCALE])

    by_group(members, fields_ref.shape[2], body)


def place_of(listed_ref, position):
    band, bands = lax.axis_index("band"), lax.axis_size("band")
    return lax.rem(listed_ref[0, position] - band + 1 + bands, bands)


def localize(rows, lon, gscale, listed_ref, counts_ref, cells_ref, near_ref, weight_ref):
    mem = lax.axis_index("mem")
    group_cells, obs_total = weight_ref.shape
    obs_rows = obs_total // LIST
    cells = cells_ref[...]
    own_lat = jnp.bitwise_and(lax.shift_right_logical(cells, 8), rows - 1).astype(F32)
    own_lon = jnp.bitwise_and(cells, lon - 1).astype(F32)

    def pair(side, slot):
        return jnp.concatenate([near_ref[side, slot : slot + 1, :], near_ref[side, slot + 1 : slot + 2, :]], axis=1)

    halves = lon // group_cells
    cell_row = (mem // halves).astype(F32)
    cell_lon = (
        lax.broadcasted_iota(jnp.int32, (group_cells, obs_rows), 0) + lax.rem(mem, halves) * group_cells
    ).astype(F32)
    lane = lax.broadcasted_iota(jnp.int32, (group_cells, obs_rows), 1)
    for position in range(LIST):
        place = place_of(listed_ref, position)
        lat = jnp.where(place == 0, pair(0, 4), jnp.where(place == 1, own_lat, pair(1, 4)))
        east = jnp.where(place == 0, pair(0, 6), jnp.where(place == 1, own_lon, pair(1, 6)))
        lat_gap = jnp.abs(lat + (place - 1).astype(F32) * rows - cell_row) * (1.0 / rows)
        lon_gap = jnp.abs(jnp.broadcast_to(east, cell_lon.shape) - cell_lon)
        lon_gap = jnp.minimum(lon_gap, lon - lon_gap) * (4.0 / lon)
        decay = jnp.exp(-0.5 * (jnp.broadcast_to(lat_gap * lat_gap, lon_gap.shape) + lon_gap * lon_gap)) * gscale
        live = lane < counts_ref[listed_ref[0, position]]
        weight_ref[:, position * obs_rows : (position + 1) * obs_rows] = jnp.where(live, decay, 0.0)


def transform(
    listed_ref, columns_ref, weight_hbm, own_ref, fetched_ref, swapped_ref, analysed_ref, observed_ref, weight_ref, sems
):
    shares, share, cells = columns_ref.shape
    obs_rows = own_ref.shape[1]
    first_core = lax.rem(lax.axis_index("mem"), 2) == 0
    copies = []
    for position in range(LIST):
        target = observed_ref.at[pl.ds(position * obs_rows, obs_rows), :]
        place = place_of(listed_ref, position)
        near = place != 1
        fetched = jnp.logical_and(near, (place == 0) == first_core)
        swapped = jnp.logical_and(near, (place == 0) != first_core)
        for chosen, source in ((place == 1, own_ref), (fetched, fetched_ref), (swapped, swapped_ref)):
            copy = pltpu.make_async_copy(source.at[0], target, sems.at[position])
            pl.when(chosen)(copy.start)
        copies.append(copy)
    weight_copy = pltpu.make_async_copy(weight_hbm, weight_ref, sems.at[LIST])
    weight_copy.start()
    columns = jnp.transpose(columns_ref[...].reshape(shares * share, cells)) * (1.0 / SEND_SCALE)
    average = jnp.mean(columns, axis=1, keepdims=True)
    series = columns - average
    combined = COEFFS[0] * series
    for copy in copies + [weight_copy]:
        copy.wait()
    for power in range(1, DEGREE + 1):
        projected = lax.dot_general(
            series.astype(BF16), observed_ref[...], (((1,), (1,)), ((), ())), preferred_element_type=F32
        )
        scaled = (projected * weight_ref[...]).astype(BF16)
        series = jnp.dot(scaled, observed_ref[...], preferred_element_type=F32)
        combined = combined + COEFFS[power] * series
    analysed = (average + combined).astype(BF16)
    analysed_ref[...] = jnp.transpose(analysed).reshape(shares, share, cells)


def unpack(members, rows, returned_ref, out_ref):
    for row in range(rows):
        for side in range(2):
            out_ref[pl.ds(side * rows + row, members, stride=2 * rows), :] = returned_ref[2 * row + side].astype(F32)


def shards(state, courant, obs_pert, obs_cell, block_rows, band_list):
    members, rows, lon = state.shape
    bands = lax.axis_size("band")
    shares = lax.axis_size("mem")
    obs_rows, all_members = obs_pert.shape[1:]
    cells = rows * lon // shares
    message = pltpu.VMEM((STEPS, members + EXTRA, lon), BF16)
    halo_scratch = [pltpu.VMEM((STEPS, members, lon), F32), pltpu.VMEM((STEPS, 4, 8, lon), F32)]
    ring = [
        (band * shares + mem, (band + (-1 if mem % 2 else 1)) % bands * shares + mem)
        for band in range(bands)
        for mem in range(shares)
    ]
    southward, northward, fields, winds = pl.pallas_call(
        functools.partial(pack, members, rows),
        out_shape=(
            message,
            message,
            pltpu.VMEM((rows, members, lon), F32),
            pltpu.VMEM((rows, 4, 8, lon), F32),
        ),
        in_specs=[HBM] * 3,
        out_specs=(VMEM,) * 4,
        scratch_shapes=[
            pltpu.VMEM((members * rows * lon // LANES, LANES), F32),
            pltpu.VMEM(courant.shape, F32),
            pltpu.VMEM(obs_cell.shape, jnp.int32),
            pltpu.SemaphoreType.DMA((3,)),
        ],
        compiler_params=PARAMS,
        name="pack",
    )(
        in_hbm(state.reshape(members, rows, lon // LANES, LANES).transpose(0, 2, 1, 3).reshape(-1, LANES)),
        in_hbm(courant),
        in_hbm(obs_cell),
    )
    above = lax.ppermute(southward, "band", [(band, (band + 1) % bands) for band in range(bands)])
    below = lax.ppermute(northward, "band", [((band + 1) % bands, band) for band in range(bands)])
    fields, winds = in_vmem(fields), in_vmem(winds)
    centre = pl.pallas_call(
        functools.partial(inner, members, rows),
        out_shape=pltpu.VMEM((len(INNER), members, lon), F32),
        in_specs=[VMEM] * 2,
        out_specs=VMEM,
        compiler_params=PARAMS,
        name="inner",
    )(fields, winds)
    centre, above = in_vmem(centre), in_vmem(above)
    north = pl.pallas_call(
        functools.partial(upper, members, rows),
        out_shape=pltpu.VMEM((len(UPPER), members, lon), F32),
        in_specs=[VMEM] * 4,
        out_specs=VMEM,
        scratch_shapes=halo_scratch,
        compiler_params=PARAMS,
        name="upper",
    )(fields, winds, centre, above)
    source, _ = lax.optimization_barrier((obs_pert, north))
    fetched = lax.ppermute(source, ("band", "mem"), ring)
    groups, near = pl.pallas_call(
        functools.partial(lower, members, rows),
        out_shape=(
            pltpu.VMEM((shares, members, cells), F32),
            jax.ShapeDtypeStruct((2, EXTRA, lon), F32),
        ),
        in_specs=[VMEM] * 6,
        out_specs=(VMEM,) * 2,
        scratch_shapes=halo_scratch,
        compiler_params=PARAMS,
        name="lower",
    )(fields, winds, centre, in_vmem(north), above, in_vmem(below))
    columns = lax.all_to_all(groups.astype(jnp.float16), "mem", split_axis=0, concat_axis=0, tiled=True)
    columns = columns.astype(F32)
    held, _ = lax.optimization_barrier((fetched, groups))
    swapped = lax.ppermute(held, "mem", [(mem, mem ^ 1) for mem in range(shares)])
    weight = pl.pallas_call(
        functools.partial(localize, rows, lon, 1.0 / (all_members + LIST * obs_rows)),
        out_shape=jax.ShapeDtypeStruct((cells, LIST * obs_rows), F32),
        in_specs=[SMEM, SMEM, VMEM, VMEM],
        out_specs=VMEM,
        compiler_params=PARAMS,
        name="localize",
    )(band_list, block_rows, obs_cell, near)
    analysed = pl.pallas_call(
        transform,
        out_shape=pltpu.VMEM((shares, members, cells), BF16),
        in_specs=[SMEM, VMEM, ANY, ANY, ANY, ANY],
        out_specs=VMEM,
        scratch_shapes=[
            pltpu.VMEM((LIST * obs_rows, all_members), BF16),
            pltpu.VMEM((cells, LIST * obs_rows), F32),
            pltpu.SemaphoreType.DMA((LIST + 1,)),
        ],
        compiler_params=PARAMS,
        name="transform",
    )(band_list, in_vmem(columns), weight, obs_pert, fetched, swapped)
    returned = lax.all_to_all(analysed, "mem", split_axis=0, concat_axis=0, tiled=True)
    out = pl.pallas_call(
        functools.partial(unpack, members, rows),
        out_shape=jax.ShapeDtypeStruct((members * 2 * rows, LANES), F32),
        in_specs=[VMEM],
        out_specs=VMEM,
        compiler_params=pltpu.CompilerParams(vmem_limit_bytes=16 << 20),
        name="unpack",
    )(in_vmem(returned))
    return out.reshape(members, 2, rows, LANES).transpose(0, 2, 1, 3).reshape(members, rows, lon)


def solution(mesh):
    return jax.shard_map(
        shards,
        mesh=mesh,
        in_specs=(
            P("mem", "band", None),
            P(None, "band", None),
            P("band", None, None),
            P("band", None),
            P(),
            P("band", None),
        ),
        out_specs=P("mem", "band", None),
        check_vma=False,
    )
```

```python
import functools

import jax
import jax.numpy as jnp
from jax import lax
from jax.experimental import pallas as pl
from jax.experimental.pallas import tpu as pltpu
from jax.sharding import PartitionSpec as P


STEPS = 6
LIST = 2
DEGREE = 4

DIFFUSION = 0.05
COEFFS = (1.0, -0.5, 0.375, -0.3125, 0.2734375)

F32 = jnp.float32
BF16 = jnp.bfloat16
VMEM = pl.BlockSpec(memory_space=pltpu.VMEM)
PARAMS = pltpu.CompilerParams(vmem_limit_bytes=16 << 20)
SMEM = pl.BlockSpec(memory_space=pltpu.SMEM)
ANY = pl.BlockSpec(memory_space=pl.ANY)
HBM = pl.BlockSpec(memory_space=pltpu.HBM)

EXTRA = 8
SEND_SCALE = 4096.0
LANES = 128


def in_vmem(x):
    return pltpu.with_memory_space_constraint(x, pltpu.VMEM)


def in_hbm(x):
    return pltpu.with_memory_space_constraint(x, pltpu.HBM)


def pack(
    members, rows, state_hbm, courant_hbm, cells_hbm, southward_ref, northward_ref, fields_ref, winds_ref,
    state_ref, courant_ref, cells_ref, sems,
):
    copies = [
        pltpu.make_async_copy(source, target, sems.at[slot])
        for slot, (source, target) in enumerate(
            ((state_hbm, state_ref), (courant_hbm, courant_ref), (cells_hbm, cells_ref))
        )
    ]
    for copy in copies:
        copy.start()
    for copy in copies[1:]:
        copy.wait()
    lon = fields_ref.shape[2]
    sides = lon // LANES
    place = lax.broadcasted_iota(jnp.int32, (EXTRA, lon), 0)
    cells = cells_ref[...]
    lat = jnp.bitwise_and(lax.shift_right_logical(cells, 8), rows - 1).astype(F32)
    east = jnp.bitwise_and(cells, lon - 1).astype(F32)
    obs = jnp.zeros((EXTRA, lon), F32)
    for slot, values in ((4, lat[:, :lon]), (5, lat[:, lon:]), (6, east[:, :lon]), (7, east[:, lon:])):
        obs = jnp.where(place == slot, values, obs)
    for message_ref, first in ((southward_ref, rows - STEPS), (northward_ref, 0)):
        for step in range(STEPS):
            extra = obs
            for wind in range(2):
                value = courant_ref[wind, first + step : first + step + 1, :]
                high = value.astype(BF16).astype(F32)
                extra = jnp.where(place == wind, high, extra)
                extra = jnp.where(place == wind + 2, value - high, extra)
            message_ref[step, members:, :] = extra.astype(BF16)
    for row in range(rows):
        keep_winds(winds_ref, row, courant_ref[0, row : row + 1, :], courant_ref[1, row : row + 1, :])
    copies[0].wait()
    for row in range(rows):
        for side in range(sides):
            lanes = slice(side * LANES, (side + 1) * LANES)
            values = state_ref[pl.ds(side * rows + row, members, stride=sides * rows), :]
            fields_ref[row, :, lanes] = values
            if row >= rows - STEPS:
                southward_ref[row - rows + STEPS, :members, lanes] = values.astype(BF16)
            if row < STEPS:
                northward_ref[row, :members, lanes] = values.astype(BF16)


def keep_winds(winds_ref, row, value0, value1):
    for wind, value in ((0, value0), (1, value1)):
        half = 0.5 * jnp.broadcast_to(value, winds_ref.shape[2:])
        winds_ref[row, 2 * wind] = half
        winds_ref[row, 2 * wind + 1] = half + DIFFUSION


def open_message(members, message_ref, halo_ref, winds_ref):
    for step in range(STEPS):
        halo_ref[step] = message_ref[step, :members, :].astype(F32)
        extra = message_ref[step, members:, :].astype(F32)
        keep_winds(winds_ref, step, extra[0:1] + extra[2:3], extra[1:2] + extra[3:4])


def minus(left, right):
    return [x - y for x, y in zip(left, right)]


def turned(parts, way, edge, lane):
    mixed = [jnp.where(lane == edge, parts[(side - way) % len(parts)], part) for side, part in enumerate(parts)]
    return [pltpu.roll(part, way % LANES, 1) for part in mixed]


def march(values, first, last, wind, lane):
    fresh = {}
    north = minus(values[first], values[first - 1])
    for row in range(first, last + 1):
        centre = values[row]
        south = minus(values[row + 1], centre)
        west = minus(centre, turned(centre, 1, LANES - 1, lane))
        east = turned(west, -1, 0, lane)
        new = []
        for side, value in enumerate(centre):
            curve = jnp.tanh(value)
            new.append(
                value
                - north[side] * (wind(row, 0, side) * curve + wind(row, 1, side))
                - west[side] * (wind(row, 2, side) * curve + wind(row, 3, side))
                + DIFFUSION * (south[side] + east[side])
            )
        fresh[row] = new
        north = south
    return fresh


def by_group(members, lon, body, size=32, unroll=1):
    lane = lax.broadcasted_iota(jnp.int32, (size, LANES), 1)
    sides = [slice(side * LANES, (side + 1) * LANES) for side in range(lon // LANES)]

    def run(index, carry):
        group = pl.ds(pl.multiple_of(index * size, size), size)

        def read(ref, row):
            return [ref[row, group, lanes] for lanes in sides]

        def write(ref, row, parts):
            for lanes, part in zip(sides, parts):
                ref[row, group, lanes] = part

        body(read, write, lane)
        return carry

    lax.fori_loop(0, members // size, run, 0, unroll=unroll)


def wind_of(size, winds_ref, halo_winds_ref=None, halo_first=0):
    def wind(row, kind, side):
        lanes = slice(side * LANES, (side + 1) * LANES)
        if 0 <= row < winds_ref.shape[0]:
            value = winds_ref[row, kind, :, lanes]
        else:
            value = halo_winds_ref[row - halo_first, kind, :, lanes]
        return jnp.concatenate([value] * (size // value.shape[0]), axis=0)

    return wind


INNER = ((1, 1), (1, 2), (1, 5), (1, 6), (2, 2), (2, 3), (2, 4), (2, 5), (3, 3), (3, 4))
UPPER = ((4, 2), (4, 3), (5, 1), (5, 2), (6, 0), (6, 1))


def inner(members, rows, fields_ref, winds_ref, inner_ref):
    def body(read, write, lane):
        values = {row: read(fields_ref, row) for row in range(rows)}
        for step in range(1, rows // 2):
            values = march(values, step, rows - 1 - step, wind_of(32, winds_ref), lane)
            for slot, (at, row) in enumerate(INNER):
                if at == step:
                    write(inner_ref, slot, values[row])

    by_group(members, fields_ref.shape[2], body)


def upper(members, rows, fields_ref, winds_ref, inner_ref, message_ref, upper_ref, halo_ref, halo_winds_ref):
    open_message(members, message_ref, halo_ref, halo_winds_ref)
    wind = wind_of(32, winds_ref, halo_winds_ref, -STEPS)

    def body(read, write, lane):
        values = {row - STEPS: read(halo_ref, row) for row in range(STEPS)}
        values.update({row: read(fields_ref, row) for row in range(2)})
        for step in range(1, STEPS + 1):
            values = march(values, step - STEPS, min(step - 1, rows - 1 - step), wind, lane)
            for row in (step, step + 1):
                if (step, row) in INNER:
                    values[row] = read(inner_ref, INNER.index((step, row)))
            for slot, (at, row) in enumerate(UPPER):
                if at == step:
                    write(upper_ref, slot, values[row])

    by_group(members, fields_ref.shape[2], body)


def lower(
    members, rows, fields_ref, winds_ref, inner_ref, upper_ref, above_ref, message_ref, groups_ref, near_ref,
    halo_ref, halo_winds_ref,
):
    near_ref[0] = above_ref[0, members:, :].astype(F32)
    near_ref[1] = message_ref[0, members:, :].astype(F32)
    open_message(members, message_ref, halo_ref, halo_winds_ref)
    wind = wind_of(16, winds_ref, halo_winds_ref, rows)
    sides = fields_ref.shape[2] // LANES

    def body(read, write, lane):
        values = {rows + row: read(halo_ref, row) for row in range(STEPS)}
        values.update({row: read(fields_ref, row) for row in (rows - 2, rows - 1)})
        for step in range(1, STEPS + 1):
            values = march(values, rows - step, rows + STEPS - 1 - step, wind, lane)
            for row in (rows - 2 - step, rows - 1 - step):
                if (step, row) in INNER:
                    values[row] = read(inner_ref, INNER.index((step, row)))
                elif (step, row) in UPPER:
                    values[row] = read(upper_ref, UPPER.index((step, row)))
        for row in range(rows):
            for side, part in enumerate(values[row]):
                write(groups_ref, sides * row + side, [part * SEND_SCALE])

    by_group(members, fields_ref.shape[2], body, 16, 2)


def place_of(listed_ref, position):
    band, bands = lax.axis_index("band"), lax.axis_size("band")
    return lax.rem(listed_ref[0, position] - band + 1 + bands, bands)


def localize(rows, lon, gscale, listed_ref, counts_ref, cells_ref, near_ref, weight_ref):
    mem = lax.axis_index("mem")
    group_cells, obs_total = weight_ref.shape
    obs_rows = obs_total // LIST
    cells = cells_ref[...]
    own_lat = jnp.bitwise_and(lax.shift_right_logical(cells, 8), rows - 1).astype(F32)
    own_lon = jnp.bitwise_and(cells, lon - 1).astype(F32)

    def pair(side, slot):
        return jnp.concatenate([near_ref[side, slot : slot + 1, :], near_ref[side, slot + 1 : slot + 2, :]], axis=1)

    halves = lon // group_cells
    cell_row = (mem // halves).astype(F32)
    cell_lon = (
        lax.broadcasted_iota(jnp.int32, (group_cells, obs_rows), 0) + lax.rem(mem, halves) * group_cells
    ).astype(F32)
    lane = lax.broadcasted_iota(jnp.int32, (group_cells, obs_rows), 1)
    for position in range(LIST):
        place = place_of(listed_ref, position)
        lat = jnp.where(place == 0, pair(0, 4), jnp.where(place == 1, own_lat, pair(1, 4)))
        east = jnp.where(place == 0, pair(0, 6), jnp.where(place == 1, own_lon, pair(1, 6)))
        lat_gap = jnp.abs(lat + (place - 1).astype(F32) * rows - cell_row) * (1.0 / rows)
        lon_gap = jnp.abs(jnp.broadcast_to(east, cell_lon.shape) - cell_lon)
        lon_gap = jnp.minimum(lon_gap, lon - lon_gap) * (4.0 / lon)
        decay = jnp.exp(-0.5 * (jnp.broadcast_to(lat_gap * lat_gap, lon_gap.shape) + lon_gap * lon_gap)) * gscale
        live = lane < counts_ref[listed_ref[0, position]]
        weight_ref[:, position * obs_rows : (position + 1) * obs_rows] = jnp.where(live, decay, 0.0)


def transform(
    listed_ref, columns_ref, weight_hbm, own_ref, fetched_ref, swapped_ref, analysed_ref,
    observed_ref, weight_ref, series_ref, scaled_ref, combined_ref, sems,
):
    shares, share, cells = columns_ref.shape
    obs_rows = own_ref.shape[1]
    first_core = lax.rem(lax.axis_index("mem"), 2) == 0
    copies = []
    for position in range(LIST):
        target = observed_ref.at[pl.ds(position * obs_rows, obs_rows), :]
        place = place_of(listed_ref, position)
        near = place != 1
        fetched = jnp.logical_and(near, (place == 0) == first_core)
        swapped = jnp.logical_and(near, (place == 0) != first_core)
        for chosen, source in ((place == 1, own_ref), (fetched, fetched_ref), (swapped, swapped_ref)):
            copy = pltpu.make_async_copy(source.at[0], target, sems.at[position])
            pl.when(chosen)(copy.start)
        copies.append(copy)
        if position == 0:
            weight_copy = pltpu.make_async_copy(weight_hbm, weight_ref, sems.at[LIST])
            weight_copy.start()
    columns = jnp.transpose(columns_ref[...].reshape(shares * share, cells)) * (1.0 / SEND_SCALE)
    average = jnp.mean(columns, axis=1, keepdims=True)
    series_ref[...] = (columns - average).astype(BF16)
    combined_ref[...] = columns
    blocks = [slice(position * obs_rows, (position + 1) * obs_rows) for position in range(LIST)]
    halves = [slice(half * obs_rows, (half + 1) * obs_rows) for half in range(shares * share // obs_rows)]
    for power in range(1, DEGREE + 1):
        for position, block in enumerate(blocks):
            if power == 1:
                copies[position].wait()
            projected = lax.dot_general(
                series_ref[...], observed_ref[block, :], (((1,), (1,)), ((), ())), preferred_element_type=F32
            )
            if power == 1 and position == 0:
                weight_copy.wait()
            scaled_ref[:, block] = (projected * weight_ref[:, block]).astype(BF16)
        for half in halves:
            series = jnp.dot(scaled_ref[...], observed_ref[:, half], preferred_element_type=F32)
            combined = combined_ref[:, half] + COEFFS[power] * series
            if power < DEGREE:
                series_ref[:, half] = series.astype(BF16)
                combined_ref[:, half] = combined
            else:
                first, last = half.start // share, half.stop // share
                analysed_ref[first:last] = jnp.transpose(combined.astype(BF16)).reshape(last - first, share, cells)


def unpack(members, rows, returned_ref, out_ref):
    for row in range(rows):
        for side in range(2):
            out_ref[pl.ds(side * rows + row, members, stride=2 * rows), :] = returned_ref[2 * row + side].astype(F32)


def shards(state, courant, obs_pert, obs_cell, block_rows, band_list):
    members, rows, lon = state.shape
    bands = lax.axis_size("band")
    shares = lax.axis_size("mem")
    obs_rows, all_members = obs_pert.shape[1:]
    cells = rows * lon // shares
    message = pltpu.VMEM((STEPS, members + EXTRA, lon), BF16)
    halo_scratch = [pltpu.VMEM((STEPS, members, lon), F32), pltpu.VMEM((STEPS, 4, 8, lon), F32)]
    ring = [
        (band * shares + mem, (band + (-1 if mem % 2 else 1)) % bands * shares + mem)
        for band in range(bands)
        for mem in range(shares)
    ]
    southward, northward, fields, winds = pl.pallas_call(
        functools.partial(pack, members, rows),
        out_shape=(
            message,
            message,
            pltpu.VMEM((rows, members, lon), F32),
            pltpu.VMEM((rows, 4, 8, lon), F32),
        ),
        in_specs=[HBM] * 3,
        out_specs=(VMEM,) * 4,
        scratch_shapes=[
            pltpu.VMEM((members * rows * lon // LANES, LANES), F32),
            pltpu.VMEM(courant.shape, F32),
            pltpu.VMEM(obs_cell.shape, jnp.int32),
            pltpu.SemaphoreType.DMA((3,)),
        ],
        compiler_params=PARAMS,
        name="pack",
    )(
        in_hbm(state.reshape(members, rows, lon // LANES, LANES).transpose(0, 2, 1, 3).reshape(-1, LANES)),
        in_hbm(courant),
        in_hbm(obs_cell),
    )
    above = lax.ppermute(southward, "band", [(band, (band + 1) % bands) for band in range(bands)])
    below = lax.ppermute(northward, "band", [((band + 1) % bands, band) for band in range(bands)])
    fields, winds = in_vmem(fields), in_vmem(winds)
    centre = pl.pallas_call(
        functools.partial(inner, members, rows),
        out_shape=pltpu.VMEM((len(INNER), members, lon), F32),
        in_specs=[VMEM] * 2,
        out_specs=VMEM,
        compiler_params=PARAMS,
        name="inner",
    )(fields, winds)
    source, _ = lax.optimization_barrier((obs_pert, centre))
    fetched = lax.ppermute(source, ("band", "mem"), ring)
    centre, above = in_vmem(centre), in_vmem(above)
    north = pl.pallas_call(
        functools.partial(upper, members, rows),
        out_shape=pltpu.VMEM((len(UPPER), members, lon), F32),
        in_specs=[VMEM] * 4,
        out_specs=VMEM,
        scratch_shapes=halo_scratch,
        compiler_params=PARAMS,
        name="upper",
    )(fields, winds, centre, above)
    groups, near = pl.pallas_call(
        functools.partial(lower, members, rows),
        out_shape=(
            pltpu.VMEM((shares, members, cells), F32),
            jax.ShapeDtypeStruct((2, EXTRA, lon), F32),
        ),
        in_specs=[VMEM] * 6,
        out_specs=(VMEM,) * 2,
        scratch_shapes=halo_scratch,
        compiler_params=PARAMS,
        name="lower",
    )(fields, winds, centre, in_vmem(north), above, in_vmem(below))
    columns = lax.all_to_all(groups.astype(jnp.float16), "mem", split_axis=0, concat_axis=0, tiled=True)
    columns = columns.astype(F32)
    held, _ = lax.optimization_barrier((fetched, groups))
    swapped = lax.ppermute(held, "mem", [(mem, mem ^ 1) for mem in range(shares)])
    weight = pl.pallas_call(
        functools.partial(localize, rows, lon, 1.0 / (all_members + LIST * obs_rows)),
        out_shape=jax.ShapeDtypeStruct((cells, LIST * obs_rows), F32),
        in_specs=[SMEM, SMEM, VMEM, VMEM],
        out_specs=VMEM,
        compiler_params=PARAMS,
        name="localize",
    )(band_list, block_rows, obs_cell, near)
    analysed = pl.pallas_call(
        transform,
        out_shape=pltpu.VMEM((shares, members, cells), BF16),
        in_specs=[SMEM, VMEM, ANY, ANY, ANY, ANY],
        out_specs=VMEM,
        scratch_shapes=[
            pltpu.VMEM((LIST * obs_rows, all_members), BF16),
            pltpu.VMEM((cells, LIST * obs_rows), F32),
            pltpu.VMEM((cells, all_members), BF16),
            pltpu.VMEM((cells, LIST * obs_rows), BF16),
            pltpu.VMEM((cells, all_members), F32),
            pltpu.SemaphoreType.DMA((LIST + 1,)),
        ],
        compiler_params=PARAMS,
        name="transform",
    )(band_list, in_vmem(columns), weight, obs_pert, fetched, swapped)
    returned = lax.all_to_all(analysed, "mem", split_axis=0, concat_axis=0, tiled=True)
    out = pl.pallas_call(
        functools.partial(unpack, members, rows),
        out_shape=jax.ShapeDtypeStruct((members * 2 * rows, LANES), F32),
        in_specs=[VMEM],
        out_specs=VMEM,
        compiler_params=pltpu.CompilerParams(vmem_limit_bytes=16 << 20),
        name="unpack",
    )(in_vmem(returned))
    return out.reshape(members, 2, rows, LANES).transpose(0, 2, 1, 3).reshape(members, rows, lon)


def solution(mesh):
    return jax.shard_map(
        shards,
        mesh=mesh,
        in_specs=(
            P("mem", "band", None),
            P(None, "band", None),
            P("band", None, None),
            P("band", None),
            P(),
            P("band", None),
        ),
        out_specs=P("mem", "band", None),
        check_vma=False,
    )
```

```python
import functools

import jax
import jax.numpy as jnp
from jax import lax
from jax.experimental import pallas as pl
from jax.experimental.pallas import tpu as pltpu
from jax.sharding import PartitionSpec as P


STEPS = 6
LIST = 2
DEGREE = 4

DIFFUSION = 0.05
COEFFS = (1.0, -0.5, 0.375, -0.3125, 0.2734375)

F32 = jnp.float32
BF16 = jnp.bfloat16
VMEM = pl.BlockSpec(memory_space=pltpu.VMEM)
PARAMS = pltpu.CompilerParams(vmem_limit_bytes=16 << 20)
SMEM = pl.BlockSpec(memory_space=pltpu.SMEM)
HBM = pl.BlockSpec(memory_space=pltpu.HBM)

EXTRA = 16
SEND_SCALE = 4096.0
PIECES = 4
LANES = 128


def in_vmem(x):
    return pltpu.with_memory_space_constraint(x, pltpu.VMEM)


def in_hbm(x):
    return pltpu.with_memory_space_constraint(x, pltpu.HBM)


def pack(
    members, rows, state_hbm, courant_hbm, cells_hbm, southward_ref, northward_ref, fields_ref, winds_ref,
    state_ref, courant_ref, cells_ref, sems,
):
    length = state_ref.shape[0] // PIECES
    small = [
        pltpu.make_async_copy(courant_hbm, courant_ref, sems.at[PIECES]),
        pltpu.make_async_copy(cells_hbm, cells_ref, sems.at[PIECES + 1]),
    ]
    copies = []
    for piece in range(PIECES):
        part = pl.ds(piece * length, length)
        copies.append(pltpu.make_async_copy(state_hbm.at[part], state_ref.at[part], sems.at[piece]))
    for copy in small + copies:
        copy.start()
    for copy in small:
        copy.wait()
    lon = fields_ref.shape[2]
    sides = lon // LANES
    place = lax.broadcasted_iota(jnp.int32, (EXTRA, lon), 0)
    cells = cells_ref[...]
    lat = jnp.bitwise_and(lax.shift_right_logical(cells, 8), rows - 1).astype(F32)
    east = jnp.bitwise_and(cells, lon - 1).astype(F32)
    obs = jnp.zeros((EXTRA, lon), F32)
    for slot, values in enumerate((lat[:, :lon], lat[:, lon:], east[:, :lon], east[:, lon:]), 2 * STEPS):
        obs = jnp.where(place == slot, values, obs)
    for message_ref, first in ((southward_ref, rows - STEPS), (northward_ref, 0)):
        extra = obs
        for step in range(STEPS):
            for wind in range(2):
                value = courant_ref[wind, first + step : first + step + 1, :]
                extra = jnp.where(place == 2 * step + wind, value, extra)
        message_ref[STEPS * members :, :] = extra.astype(BF16)
    for row in range(rows):
        keep_winds(winds_ref, row, courant_ref[0, row : row + 1, :], courant_ref[1, row : row + 1, :])
    share = members // PIECES
    for piece in range(PIECES):
        copies[piece].wait()
        first = piece * share
        for row in range(rows):
            for side in range(sides):
                lanes = slice(side * LANES, (side + 1) * LANES)
                values = state_ref[pl.ds((first * sides + side) * rows + row, share, stride=sides * rows), :]
                fields_ref[row, first : first + share, lanes] = values
                for message_ref, step in ((southward_ref, row - rows + STEPS), (northward_ref, row)):
                    if 0 <= step < STEPS:
                        at = step * members + first
                        message_ref[at : at + share, lanes] = values.astype(BF16)


def keep_winds(winds_ref, row, value0, value1):
    for wind, value in ((0, value0), (1, value1)):
        half = 0.5 * jnp.broadcast_to(value, winds_ref.shape[2:])
        winds_ref[row, 2 * wind] = half
        winds_ref[row, 2 * wind + 1] = half + DIFFUSION


def open_message(members, message_ref, halo_ref, winds_ref):
    extra = message_ref[STEPS * members :, :].astype(F32)
    for step in range(STEPS):
        halo_ref[step] = message_ref[step * members : (step + 1) * members, :].astype(F32)
        keep_winds(winds_ref, step, extra[2 * step : 2 * step + 1], extra[2 * step + 1 : 2 * step + 2])


def minus(left, right):
    return [x - y for x, y in zip(left, right)]


def turned(parts, way, edge, lane):
    mixed = [jnp.where(lane == edge, parts[(side - way) % len(parts)], part) for side, part in enumerate(parts)]
    return [pltpu.roll(part, way % LANES, 1) for part in mixed]


def march(values, first, last, wind, lane):
    fresh = {}
    north = minus(values[first], values[first - 1])
    for row in range(first, last + 1):
        centre = values[row]
        south = minus(values[row + 1], centre)
        west = minus(centre, turned(centre, 1, LANES - 1, lane))
        east = turned(west, -1, 0, lane)
        new = []
        for side, value in enumerate(centre):
            curve = jnp.tanh(value)
            new.append(
                value
                - north[side] * (wind(row, 0, side) * curve + wind(row, 1, side))
                - west[side] * (wind(row, 2, side) * curve + wind(row, 3, side))
                + DIFFUSION * (south[side] + east[side])
            )
        fresh[row] = new
        north = south
    return fresh


def by_group(members, lon, body, size=32, unroll=1):
    lane = lax.broadcasted_iota(jnp.int32, (size, LANES), 1)
    sides = [slice(side * LANES, (side + 1) * LANES) for side in range(lon // LANES)]

    def run(index, carry):
        group = pl.ds(pl.multiple_of(index * size, size), size)

        def read(ref, row):
            return [ref[row, group, lanes] for lanes in sides]

        def write(ref, row, parts):
            for lanes, part in zip(sides, parts):
                ref[row, group, lanes] = part

        body(read, write, lane)
        return carry

    lax.fori_loop(0, members // size, run, 0, unroll=unroll)


def wind_of(size, winds_ref, halo_winds_ref=None, halo_first=0):
    def wind(row, kind, side):
        lanes = slice(side * LANES, (side + 1) * LANES)
        if 0 <= row < winds_ref.shape[0]:
            value = winds_ref[row, kind, :, lanes]
        else:
            value = halo_winds_ref[row - halo_first, kind, :, lanes]
        return jnp.concatenate([value] * (size // value.shape[0]), axis=0)

    return wind


INNER = ((1, 1), (1, 2), (1, 5), (1, 6), (2, 2), (2, 3), (2, 4), (2, 5), (3, 3), (3, 4))
UPPER = ((4, 2), (4, 3), (5, 1), (5, 2), (6, 0), (6, 1))


def inner(members, rows, fields_ref, winds_ref, inner_ref):
    def body(read, write, lane):
        values = {row: read(fields_ref, row) for row in range(rows)}
        for step in range(1, rows // 2):
            values = march(values, step, rows - 1 - step, wind_of(32, winds_ref), lane)
            for slot, (at, row) in enumerate(INNER):
                if at == step:
                    write(inner_ref, slot, values[row])

    by_group(members, fields_ref.shape[2], body)


def upper(members, rows, fields_ref, winds_ref, inner_ref, message_ref, upper_ref, halo_ref, halo_winds_ref):
    open_message(members, message_ref, halo_ref, halo_winds_ref)
    wind = wind_of(32, winds_ref, halo_winds_ref, -STEPS)

    def body(read, write, lane):
        values = {row - STEPS: read(halo_ref, row) for row in range(STEPS)}
        values.update({row: read(fields_ref, row) for row in range(2)})
        for step in range(1, STEPS + 1):
            values = march(values, step - STEPS, min(step - 1, rows - 1 - step), wind, lane)
            for row in (step, step + 1):
                if (step, row) in INNER:
                    values[row] = read(inner_ref, INNER.index((step, row)))
            for slot, (at, row) in enumerate(UPPER):
                if at == step:
                    write(upper_ref, slot, values[row])

    by_group(members, fields_ref.shape[2], body)


def lower(
    members, rows, fields_ref, winds_ref, inner_ref, upper_ref, above_ref, message_ref, groups_ref, near_ref,
    halo_ref, halo_winds_ref,
):
    for side, ref in enumerate((above_ref, message_ref)):
        near_ref[side] = ref[STEPS * members :, :].astype(F32)
    open_message(members, message_ref, halo_ref, halo_winds_ref)
    wind = wind_of(16, winds_ref, halo_winds_ref, rows)
    sides = fields_ref.shape[2] // LANES

    def body(read, write, lane):
        values = {rows + row: read(halo_ref, row) for row in range(STEPS)}
        values.update({row: read(fields_ref, row) for row in (rows - 2, rows - 1)})
        for step in range(1, STEPS + 1):
            values = march(values, rows - step, rows + STEPS - 1 - step, wind, lane)
            for row in (rows - 2 - step, rows - 1 - step):
                if (step, row) in INNER:
                    values[row] = read(inner_ref, INNER.index((step, row)))
                elif (step, row) in UPPER:
                    values[row] = read(upper_ref, UPPER.index((step, row)))
        for row in range(rows):
            for side, part in enumerate(values[row]):
                write(groups_ref, sides * row + side, [part * SEND_SCALE])

    by_group(members, fields_ref.shape[2], body, 16, 2)


def place_of(listed_ref, position):
    band, bands = lax.axis_index("band"), lax.axis_size("band")
    return lax.rem(listed_ref[0, position] - band + 1 + bands, bands)


def localize(rows, lon, gscale, listed_ref, counts_ref, cells_ref, near_ref, weight_ref):
    mem = lax.axis_index("mem")
    group_cells, obs_total = weight_ref.shape
    obs_rows = obs_total // LIST
    cells = cells_ref[...]
    own_lat = jnp.bitwise_and(lax.shift_right_logical(cells, 8), rows - 1).astype(F32)
    own_lon = jnp.bitwise_and(cells, lon - 1).astype(F32)

    def pair(side, slot):
        return jnp.concatenate([near_ref[side, slot : slot + 1, :], near_ref[side, slot + 1 : slot + 2, :]], axis=1)

    halves = lon // group_cells
    cell_row = (mem // halves).astype(F32)
    cell_lon = (
        lax.broadcasted_iota(jnp.int32, (group_cells, obs_rows), 0) + lax.rem(mem, halves) * group_cells
    ).astype(F32)
    lane = lax.broadcasted_iota(jnp.int32, (group_cells, obs_rows), 1)
    for position in range(LIST):
        place = place_of(listed_ref, position)
        lat = jnp.where(place == 0, pair(0, 2 * STEPS), jnp.where(place == 1, own_lat, pair(1, 2 * STEPS)))
        east = jnp.where(place == 0, pair(0, 2 * STEPS + 2), jnp.where(place == 1, own_lon, pair(1, 2 * STEPS + 2)))
        lat_gap = jnp.abs(lat + (place - 1).astype(F32) * rows - cell_row) * (1.0 / rows)
        lon_gap = jnp.abs(jnp.broadcast_to(east, cell_lon.shape) - cell_lon)
        lon_gap = jnp.minimum(lon_gap, lon - lon_gap) * (4.0 / lon)
        decay = jnp.exp(-0.5 * (jnp.broadcast_to(lat_gap * lat_gap, lon_gap.shape) + lon_gap * lon_gap)) * gscale
        live = lane < counts_ref[listed_ref[0, position]]
        weight_ref[:, position * obs_rows : (position + 1) * obs_rows] = jnp.where(live, decay, 0.0)


def transform(
    listed_ref, columns_ref, weight_ref, own_ref, fetched_ref, swapped_hbm, analysed_ref,
    observed_ref, series_ref, scaled_ref, combined_ref, sems,
):
    shares, share, cells = columns_ref.shape
    obs_rows = own_ref.shape[1]
    first_core = lax.rem(lax.axis_index("mem"), 2) == 0
    blocks = [slice(position * obs_rows, (position + 1) * obs_rows) for position in range(LIST)]
    halves = [slice(half * obs_rows, (half + 1) * obs_rows) for half in range(shares * share // obs_rows)]

    def take(source_ref, block):
        def copy():
            observed_ref[block, :] = source_ref[0]

        return copy

    waits = []
    for position, block in enumerate(blocks):
        place = place_of(listed_ref, position)
        swapped = jnp.logical_and(place != 1, (place == 0) != first_core)
        copy = pltpu.make_async_copy(swapped_hbm.at[0], observed_ref.at[block, :], sems.at[position])
        pl.when(swapped)(copy.start)
        waits.append((swapped, copy.wait))
    for position, block in enumerate(blocks):
        place = place_of(listed_ref, position)
        pl.when(place == 1)(take(own_ref, block))
        pl.when(jnp.logical_and(place != 1, (place == 0) == first_core))(take(fetched_ref, block))
    columns = jnp.transpose(columns_ref[...].reshape(shares * share, cells)) * (1.0 / SEND_SCALE)
    average = jnp.mean(columns, axis=1, keepdims=True)
    series_ref[...] = (columns - average).astype(BF16)
    combined_ref[...] = columns
    for power in range(1, DEGREE + 1):
        for (swapped, wait), block in zip(waits, blocks):
            if power == 1:
                pl.when(swapped)(wait)
            projected = lax.dot_general(
                series_ref[...], observed_ref[block, :], (((1,), (1,)), ((), ())), preferred_element_type=F32
            )
            scaled_ref[:, block] = (projected * weight_ref[:, block]).astype(BF16)
        for half in halves:
            series = jnp.dot(scaled_ref[...], observed_ref[:, half], preferred_element_type=F32)
            combined = combined_ref[:, half] + COEFFS[power] * series
            if power < DEGREE:
                series_ref[:, half] = series.astype(BF16)
                combined_ref[:, half] = combined
            else:
                first, last = half.start // share, half.stop // share
                analysed_ref[first:last] = jnp.transpose(combined.astype(BF16)).reshape(last - first, share, cells)


def unpack(members, rows, returned_ref, out_ref):
    for row in range(rows):
        for side in range(2):
            out_ref[pl.ds(side * rows + row, members, stride=2 * rows), :] = returned_ref[2 * row + side].astype(F32)


def shards(state, courant, obs_pert, obs_cell, block_rows, band_list):
    members, rows, lon = state.shape
    bands = lax.axis_size("band")
    shares = lax.axis_size("mem")
    obs_rows, all_members = obs_pert.shape[1:]
    cells = rows * lon // shares
    message = pltpu.VMEM((STEPS * members + EXTRA, lon), BF16)
    halo_scratch = [pltpu.VMEM((STEPS, members, lon), F32), pltpu.VMEM((STEPS, 4, 8, lon), F32)]
    ring = [
        (band * shares + mem, (band + (-1 if mem % 2 else 1)) % bands * shares + mem)
        for band in range(bands)
        for mem in range(shares)
    ]
    southward, northward, fields, winds = pl.pallas_call(
        functools.partial(pack, members, rows),
        out_shape=(
            message,
            message,
            pltpu.VMEM((rows, members, lon), F32),
            pltpu.VMEM((rows, 4, 8, lon), F32),
        ),
        in_specs=[HBM] * 3,
        out_specs=(VMEM,) * 4,
        scratch_shapes=[
            pltpu.VMEM((members * rows * lon // LANES, LANES), F32),
            pltpu.VMEM(courant.shape, F32),
            pltpu.VMEM(obs_cell.shape, jnp.int32),
            pltpu.SemaphoreType.DMA((PIECES + 2,)),
        ],
        compiler_params=PARAMS,
        name="pack",
    )(
        in_hbm(state.reshape(members, rows, lon // LANES, LANES).transpose(0, 2, 1, 3).reshape(-1, LANES)),
        in_hbm(courant),
        in_hbm(obs_cell),
    )
    above = lax.ppermute(southward, "band", [(band, (band + 1) % bands) for band in range(bands)])
    below = lax.ppermute(northward, "band", [((band + 1) % bands, band) for band in range(bands)])
    fields, winds = in_vmem(fields), in_vmem(winds)
    centre = pl.pallas_call(
        functools.partial(inner, members, rows),
        out_shape=pltpu.VMEM((len(INNER), members, lon), F32),
        in_specs=[VMEM] * 2,
        out_specs=VMEM,
        compiler_params=PARAMS,
        name="inner",
    )(fields, winds)
    source, _ = lax.optimization_barrier((obs_pert, centre))
    fetched = lax.ppermute(source, ("band", "mem"), ring)
    centre, above = in_vmem(centre), in_vmem(above)
    north = pl.pallas_call(
        functools.partial(upper, members, rows),
        out_shape=pltpu.VMEM((len(UPPER), members, lon), F32),
        in_specs=[VMEM] * 4,
        out_specs=VMEM,
        scratch_shapes=halo_scratch,
        compiler_params=PARAMS,
        name="upper",
    )(fields, winds, centre, above)
    groups, near = pl.pallas_call(
        functools.partial(lower, members, rows),
        out_shape=(
            pltpu.VMEM((shares, members, cells), F32),
            jax.ShapeDtypeStruct((2, EXTRA, lon), F32),
        ),
        in_specs=[VMEM] * 6,
        out_specs=(VMEM,) * 2,
        scratch_shapes=halo_scratch,
        compiler_params=PARAMS,
        name="lower",
    )(fields, winds, centre, in_vmem(north), above, in_vmem(below))
    columns = lax.all_to_all(groups.astype(jnp.float16), "mem", split_axis=0, concat_axis=0, tiled=True)
    columns = columns.astype(F32)
    held, _ = lax.optimization_barrier((fetched, groups))
    swapped = lax.ppermute(held, "mem", [(mem, mem ^ 1) for mem in range(shares)])
    weight = pl.pallas_call(
        functools.partial(localize, rows, lon, 1.0 / (all_members + LIST * obs_rows)),
        out_shape=pltpu.VMEM((cells, LIST * obs_rows), F32),
        in_specs=[SMEM, SMEM, VMEM, VMEM],
        out_specs=VMEM,
        compiler_params=PARAMS,
        name="localize",
    )(band_list, block_rows, obs_cell, near)
    analysed = pl.pallas_call(
        transform,
        out_shape=pltpu.VMEM((shares, members, cells), BF16),
        in_specs=[SMEM] + [VMEM] * 4 + [HBM],
        out_specs=VMEM,
        scratch_shapes=[
            pltpu.VMEM((LIST * obs_rows, all_members), BF16),
            pltpu.VMEM((cells, all_members), BF16),
            pltpu.VMEM((cells, LIST * obs_rows), BF16),
            pltpu.VMEM((cells, all_members), F32),
            pltpu.SemaphoreType.DMA((LIST,)),
        ],
        compiler_params=PARAMS,
        name="transform",
    )(band_list, *[in_vmem(x) for x in (columns, weight, obs_pert, fetched)], in_hbm(swapped))
    returned = lax.all_to_all(analysed, "mem", split_axis=0, concat_axis=0, tiled=True)
    out = pl.pallas_call(
        functools.partial(unpack, members, rows),
        out_shape=jax.ShapeDtypeStruct((members * 2 * rows, LANES), F32),
        in_specs=[VMEM],
        out_specs=VMEM,
        compiler_params=pltpu.CompilerParams(vmem_limit_bytes=16 << 20),
        name="unpack",
    )(in_vmem(returned))
    return out.reshape(members, 2, rows, LANES).transpose(0, 2, 1, 3).reshape(members, rows, lon)


def solution(mesh):
    return jax.shard_map(
        shards,
        mesh=mesh,
        in_specs=(
            P("mem", "band", None),
            P(None, "band", None),
            P("band", None, None),
            P("band", None),
            P(),
            P("band", None),
        ),
        out_specs=P("mem", "band", None),
        check_vma=False,
    )
```

```python
import functools

import jax
import jax.numpy as jnp
from jax import lax
from jax.experimental import pallas as pl
from jax.experimental.pallas import tpu as pltpu
from jax.sharding import PartitionSpec as P


STEPS = 6
LIST = 2
DEGREE = 4

DIFFUSION = 0.05
COEFFS = (1.0, -0.5, 0.375, -0.3125, 0.2734375)

F32 = jnp.float32
BF16 = jnp.bfloat16
VMEM = pl.BlockSpec(memory_space=pltpu.VMEM)
PARAMS = pltpu.CompilerParams(vmem_limit_bytes=16 << 20)
SMEM = pl.BlockSpec(memory_space=pltpu.SMEM)
HBM = pl.BlockSpec(memory_space=pltpu.HBM)

EXTRA = 16
SEND_SCALE = 4096.0
PIECES = 4
LANES = 128


def in_vmem(x):
    return pltpu.with_memory_space_constraint(x, pltpu.VMEM)


def in_hbm(x):
    return pltpu.with_memory_space_constraint(x, pltpu.HBM)


def pack(
    members, rows, state_hbm, courant_hbm, cells_hbm, southward_ref, northward_ref, fields_ref, winds_ref,
    state_ref, courant_ref, cells_ref, sems,
):
    length = state_ref.shape[0] // PIECES
    small = [
        pltpu.make_async_copy(courant_hbm, courant_ref, sems.at[PIECES]),
        pltpu.make_async_copy(cells_hbm, cells_ref, sems.at[PIECES + 1]),
    ]
    copies = []
    for piece in range(PIECES):
        part = pl.ds(piece * length, length)
        copies.append(pltpu.make_async_copy(state_hbm.at[part], state_ref.at[part], sems.at[piece]))
    for copy in small + copies:
        copy.start()
    for copy in small:
        copy.wait()
    lon = fields_ref.shape[2]
    sides = lon // LANES
    place = lax.broadcasted_iota(jnp.int32, (EXTRA, lon), 0)
    cells = cells_ref[...]
    lat = jnp.bitwise_and(lax.shift_right_logical(cells, 8), rows - 1).astype(F32)
    east = jnp.bitwise_and(cells, lon - 1).astype(F32)
    obs = jnp.zeros((EXTRA, lon), F32)
    for slot, values in enumerate((lat[:, :lon], lat[:, lon:], east[:, :lon], east[:, lon:]), 2 * STEPS):
        obs = jnp.where(place == slot, values, obs)
    for message_ref, first in ((southward_ref, rows - STEPS), (northward_ref, 0)):
        extra = obs
        for step in range(STEPS):
            for wind in range(2):
                value = courant_ref[wind, first + step : first + step + 1, :]
                extra = jnp.where(place == 2 * step + wind, value, extra)
        message_ref[STEPS * members :, :] = extra.astype(BF16)
    for row in range(rows):
        keep_winds(winds_ref, row, courant_ref[0, row : row + 1, :], courant_ref[1, row : row + 1, :])
    share = members // PIECES
    for piece in range(PIECES):
        copies[piece].wait()
        first = piece * share
        for row in range(rows):
            for side in range(sides):
                lanes = slice(side * LANES, (side + 1) * LANES)
                values = state_ref[pl.ds((first * sides + side) * rows + row, share, stride=sides * rows), :]
                fields_ref[row, first : first + share, lanes] = values
                for message_ref, step in ((southward_ref, row - rows + STEPS), (northward_ref, row)):
                    if 0 <= step < STEPS:
                        at = step * members + first
                        message_ref[at : at + share, lanes] = values.astype(BF16)


def keep_winds(winds_ref, row, value0, value1):
    for wind, value in ((0, value0), (1, value1)):
        half = 0.5 * jnp.broadcast_to(value, winds_ref.shape[2:])
        winds_ref[row, 2 * wind] = half
        winds_ref[row, 2 * wind + 1] = half + DIFFUSION


def open_message(members, message_ref, halo_ref, winds_ref):
    extra = message_ref[STEPS * members :, :].astype(F32)
    for step in range(STEPS):
        halo_ref[step] = message_ref[step * members : (step + 1) * members, :].astype(F32)
        keep_winds(winds_ref, step, extra[2 * step : 2 * step + 1], extra[2 * step + 1 : 2 * step + 2])


def minus(left, right):
    return [x - y for x, y in zip(left, right)]


def turned(parts, way, edge, lane):
    mixed = [jnp.where(lane == edge, parts[(side - way) % len(parts)], part) for side, part in enumerate(parts)]
    return [pltpu.roll(part, way % LANES, 1) for part in mixed]


def march(values, first, last, wind, lane):
    fresh = {}
    north = minus(values[first], values[first - 1])
    for row in range(first, last + 1):
        centre = values[row]
        south = minus(values[row + 1], centre)
        west = minus(centre, turned(centre, 1, LANES - 1, lane))
        east = turned(west, -1, 0, lane)
        new = []
        for side, value in enumerate(centre):
            curve = jnp.tanh(value)
            new.append(
                value
                - north[side] * (wind(row, 0, side) * curve + wind(row, 1, side))
                - west[side] * (wind(row, 2, side) * curve + wind(row, 3, side))
                + DIFFUSION * (south[side] + east[side])
            )
        fresh[row] = new
        north = south
    return fresh


def by_group(members, lon, body, size=32, unroll=1):
    lane = lax.broadcasted_iota(jnp.int32, (size, LANES), 1)
    sides = [slice(side * LANES, (side + 1) * LANES) for side in range(lon // LANES)]

    def run(index, carry):
        group = pl.ds(pl.multiple_of(index * size, size), size)

        def read(ref, row):
            return [ref[row, group, lanes] for lanes in sides]

        def write(ref, row, parts):
            for lanes, part in zip(sides, parts):
                ref[row, group, lanes] = part

        body(read, write, lane)
        return carry

    lax.fori_loop(0, members // size, run, 0, unroll=unroll)


def wind_of(size, winds_ref, halo_winds_ref=None, halo_first=0):
    def wind(row, kind, side):
        lanes = slice(side * LANES, (side + 1) * LANES)
        if 0 <= row < winds_ref.shape[0]:
            value = winds_ref[row, kind, :, lanes]
        else:
            value = halo_winds_ref[row - halo_first, kind, :, lanes]
        return jnp.concatenate([value] * (size // value.shape[0]), axis=0)

    return wind


INNER = ((1, 1), (1, 2), (1, 5), (1, 6), (2, 2), (2, 3), (2, 4), (2, 5), (3, 3), (3, 4))
UPPER = ((4, 2), (4, 3), (5, 1), (5, 2), (6, 0), (6, 1))


def inner(members, rows, fields_ref, winds_ref, inner_ref):
    def body(read, write, lane):
        values = {row: read(fields_ref, row) for row in range(rows)}
        for step in range(1, rows // 2):
            values = march(values, step, rows - 1 - step, wind_of(32, winds_ref), lane)
            for slot, (at, row) in enumerate(INNER):
                if at == step:
                    write(inner_ref, slot, values[row])

    by_group(members, fields_ref.shape[2], body)


def upper(members, rows, fields_ref, winds_ref, inner_ref, message_ref, upper_ref, halo_ref, halo_winds_ref):
    open_message(members, message_ref, halo_ref, halo_winds_ref)
    wind = wind_of(32, winds_ref, halo_winds_ref, -STEPS)

    def body(read, write, lane):
        values = {row - STEPS: read(halo_ref, row) for row in range(STEPS)}
        values.update({row: read(fields_ref, row) for row in range(2)})
        for step in range(1, STEPS + 1):
            values = march(values, step - STEPS, min(step - 1, rows - 1 - step), wind, lane)
            for row in (step, step + 1):
                if (step, row) in INNER:
                    values[row] = read(inner_ref, INNER.index((step, row)))
            for slot, (at, row) in enumerate(UPPER):
                if at == step:
                    write(upper_ref, slot, values[row])

    by_group(members, fields_ref.shape[2], body)


def lower(
    members, rows, fields_ref, winds_ref, inner_ref, upper_ref, above_ref, message_ref, groups_ref, near_ref,
    halo_ref, halo_winds_ref,
):
    for side, ref in enumerate((above_ref, message_ref)):
        near_ref[side] = ref[STEPS * members :, :].astype(F32)
    open_message(members, message_ref, halo_ref, halo_winds_ref)
    wind = wind_of(16, winds_ref, halo_winds_ref, rows)
    sides = fields_ref.shape[2] // LANES

    def body(read, write, lane):
        values = {rows + row: read(halo_ref, row) for row in range(STEPS)}
        values.update({row: read(fields_ref, row) for row in (rows - 2, rows - 1)})
        for step in range(1, STEPS + 1):
            values = march(values, rows - step, rows + STEPS - 1 - step, wind, lane)
            for row in (rows - 2 - step, rows - 1 - step):
                if (step, row) in INNER:
                    values[row] = read(inner_ref, INNER.index((step, row)))
                elif (step, row) in UPPER:
                    values[row] = read(upper_ref, UPPER.index((step, row)))
        for row in range(rows):
            for side, part in enumerate(values[row]):
                write(groups_ref, sides * row + side, [part * SEND_SCALE])

    by_group(members, fields_ref.shape[2], body, 16, 2)


def place_of(listed_ref, position):
    band, bands = lax.axis_index("band"), lax.axis_size("band")
    return lax.rem(listed_ref[0, position] - band + 1 + bands, bands)


def localize(rows, lon, gscale, listed_ref, counts_ref, cells_ref, near_ref, weight_ref):
    mem = lax.axis_index("mem")
    group_cells, obs_total = weight_ref.shape
    obs_rows = obs_total // LIST
    cells = cells_ref[...]
    own_lat = jnp.bitwise_and(lax.shift_right_logical(cells, 8), rows - 1).astype(F32)
    own_lon = jnp.bitwise_and(cells, lon - 1).astype(F32)

    def pair(side, slot):
        return jnp.concatenate([near_ref[side, slot : slot + 1, :], near_ref[side, slot + 1 : slot + 2, :]], axis=1)

    halves = lon // group_cells
    cell_row = (mem // halves).astype(F32)
    cell_lon = (
        lax.broadcasted_iota(jnp.int32, (group_cells, obs_rows), 0) + lax.rem(mem, halves) * group_cells
    ).astype(F32)
    lane = lax.broadcasted_iota(jnp.int32, (group_cells, obs_rows), 1)
    for position in range(LIST):
        place = place_of(listed_ref, position)
        lat = jnp.where(place == 0, pair(0, 2 * STEPS), jnp.where(place == 1, own_lat, pair(1, 2 * STEPS)))
        east = jnp.where(place == 0, pair(0, 2 * STEPS + 2), jnp.where(place == 1, own_lon, pair(1, 2 * STEPS + 2)))
        lat_gap = jnp.abs(lat + (place - 1).astype(F32) * rows - cell_row) * (1.0 / rows)
        lon_gap = jnp.abs(jnp.broadcast_to(east, cell_lon.shape) - cell_lon)
        lon_gap = jnp.minimum(lon_gap, lon - lon_gap) * (4.0 / lon)
        decay = jnp.exp(-0.5 * (jnp.broadcast_to(lat_gap * lat_gap, lon_gap.shape) + lon_gap * lon_gap)) * gscale
        live = lane < counts_ref[listed_ref[0, position]]
        weight_ref[:, position * obs_rows : (position + 1) * obs_rows] = jnp.where(live, decay, 0.0)


def transform(
    listed_ref, columns_ref, weight_ref, own_ref, fetched_ref, swapped_hbm, analysed_ref,
    observed_ref, series_ref, scaled_ref, combined_ref, sems,
):
    shares, share, cells = columns_ref.shape
    obs_rows = own_ref.shape[1]
    first_core = lax.rem(lax.axis_index("mem"), 2) == 0
    blocks = [slice(position * obs_rows, (position + 1) * obs_rows) for position in range(LIST)]
    halves = [slice(half * obs_rows, (half + 1) * obs_rows) for half in range(shares * share // obs_rows)]

    def take(source_ref, block):
        def copy():
            observed_ref[block, :] = source_ref[0]

        return copy

    waits = []
    for position, block in enumerate(blocks):
        place = place_of(listed_ref, position)
        swapped = jnp.logical_and(place != 1, (place == 0) != first_core)
        copy = pltpu.make_async_copy(swapped_hbm.at[0], observed_ref.at[block, :], sems.at[position])
        pl.when(swapped)(copy.start)
        waits.append((swapped, copy.wait))
    for position, block in enumerate(blocks):
        place = place_of(listed_ref, position)
        pl.when(place == 1)(take(own_ref, block))
        pl.when(jnp.logical_and(place != 1, (place == 0) == first_core))(take(fetched_ref, block))
    columns = jnp.transpose(columns_ref[...].reshape(shares * share, cells)) * (1.0 / SEND_SCALE)
    average = jnp.mean(columns, axis=1, keepdims=True)
    series_ref[...] = (columns - average).astype(BF16)
    combined_ref[...] = columns
    for power in range(1, DEGREE + 1):
        for (swapped, wait), block in zip(waits, blocks):
            if power == 1:
                pl.when(swapped)(wait)
            projected = lax.dot_general(
                series_ref[...], observed_ref[block, :], (((1,), (1,)), ((), ())), preferred_element_type=F32
            )
            scaled_ref[:, block] = (projected * weight_ref[:, block]).astype(BF16)
        for half in halves:
            series = jnp.dot(scaled_ref[...], observed_ref[:, half], preferred_element_type=F32)
            combined = combined_ref[:, half] + COEFFS[power] * series
            if power < DEGREE:
                series_ref[:, half] = series.astype(BF16)
                combined_ref[:, half] = combined
            else:
                first, last = half.start // share, half.stop // share
                analysed_ref[first:last] = jnp.transpose(combined.astype(BF16)).reshape(last - first, share, cells)


def unpack(members, rows, returned_ref, out_hbm, out_ref, sems):
    share = members // PIECES
    length = out_ref.shape[0] // PIECES
    copies = []
    for piece in range(PIECES):
        first = piece * share
        for row in range(rows):
            for side in range(2):
                out_ref[pl.ds((first * 2 + side) * rows + row, share, stride=2 * rows), :] = returned_ref[
                    2 * row + side, first : first + share, :
                ].astype(F32)
        part = pl.ds(piece * length, length)
        copies.append(pltpu.make_async_copy(out_ref.at[part], out_hbm.at[part], sems.at[piece]))
        copies[-1].start()
    for copy in copies:
        copy.wait()


def shards(state, courant, obs_pert, obs_cell, block_rows, band_list):
    members, rows, lon = state.shape
    bands = lax.axis_size("band")
    shares = lax.axis_size("mem")
    obs_rows, all_members = obs_pert.shape[1:]
    cells = rows * lon // shares
    message = pltpu.VMEM((STEPS * members + EXTRA, lon), BF16)
    halo_scratch = [pltpu.VMEM((STEPS, members, lon), F32), pltpu.VMEM((STEPS, 4, 8, lon), F32)]
    ring = [
        (band * shares + mem, (band + (-1 if mem % 2 else 1)) % bands * shares + mem)
        for band in range(bands)
        for mem in range(shares)
    ]
    southward, northward, fields, winds = pl.pallas_call(
        functools.partial(pack, members, rows),
        out_shape=(
            message,
            message,
            pltpu.VMEM((rows, members, lon), F32),
            pltpu.VMEM((rows, 4, 8, lon), F32),
        ),
        in_specs=[HBM] * 3,
        out_specs=(VMEM,) * 4,
        scratch_shapes=[
            pltpu.VMEM((members * rows * lon // LANES, LANES), F32),
            pltpu.VMEM(courant.shape, F32),
            pltpu.VMEM(obs_cell.shape, jnp.int32),
            pltpu.SemaphoreType.DMA((PIECES + 2,)),
        ],
        compiler_params=PARAMS,
        name="pack",
    )(
        in_hbm(state.reshape(members, rows, lon // LANES, LANES).transpose(0, 2, 1, 3).reshape(-1, LANES)),
        in_hbm(courant),
        in_hbm(obs_cell),
    )
    above = lax.ppermute(southward, "band", [(band, (band + 1) % bands) for band in range(bands)])
    below = lax.ppermute(northward, "band", [((band + 1) % bands, band) for band in range(bands)])
    fields, winds = in_vmem(fields), in_vmem(winds)
    centre = pl.pallas_call(
        functools.partial(inner, members, rows),
        out_shape=pltpu.VMEM((len(INNER), members, lon), F32),
        in_specs=[VMEM] * 2,
        out_specs=VMEM,
        compiler_params=PARAMS,
        name="inner",
    )(fields, winds)
    source, _ = lax.optimization_barrier((obs_pert, centre))
    fetched = lax.ppermute(source, ("band", "mem"), ring)
    centre, above = in_vmem(centre), in_vmem(above)
    north = pl.pallas_call(
        functools.partial(upper, members, rows),
        out_shape=pltpu.VMEM((len(UPPER), members, lon), F32),
        in_specs=[VMEM] * 4,
        out_specs=VMEM,
        scratch_shapes=halo_scratch,
        compiler_params=PARAMS,
        name="upper",
    )(fields, winds, centre, above)
    groups, near = pl.pallas_call(
        functools.partial(lower, members, rows),
        out_shape=(
            pltpu.VMEM((shares, members, cells), F32),
            jax.ShapeDtypeStruct((2, EXTRA, lon), F32),
        ),
        in_specs=[VMEM] * 6,
        out_specs=(VMEM,) * 2,
        scratch_shapes=halo_scratch,
        compiler_params=PARAMS,
        name="lower",
    )(fields, winds, centre, in_vmem(north), above, in_vmem(below))
    columns = lax.all_to_all(groups.astype(jnp.float16), "mem", split_axis=0, concat_axis=0, tiled=True)
    columns = columns.astype(F32)
    held, _ = lax.optimization_barrier((fetched, groups))
    swapped = lax.ppermute(held, "mem", [(mem, mem ^ 1) for mem in range(shares)])
    weight = pl.pallas_call(
        functools.partial(localize, rows, lon, 1.0 / (all_members + LIST * obs_rows)),
        out_shape=pltpu.VMEM((cells, LIST * obs_rows), F32),
        in_specs=[SMEM, SMEM, VMEM, VMEM],
        out_specs=VMEM,
        compiler_params=PARAMS,
        name="localize",
    )(band_list, block_rows, obs_cell, near)
    analysed = pl.pallas_call(
        transform,
        out_shape=pltpu.VMEM((shares, members, cells), BF16),
        in_specs=[SMEM] + [VMEM] * 4 + [HBM],
        out_specs=VMEM,
        scratch_shapes=[
            pltpu.VMEM((LIST * obs_rows, all_members), BF16),
            pltpu.VMEM((cells, all_members), BF16),
            pltpu.VMEM((cells, LIST * obs_rows), BF16),
            pltpu.VMEM((cells, all_members), F32),
            pltpu.SemaphoreType.DMA((LIST,)),
        ],
        compiler_params=PARAMS,
        name="transform",
    )(band_list, *[in_vmem(x) for x in (columns, weight, obs_pert, fetched)], in_hbm(swapped))
    returned = lax.all_to_all(analysed, "mem", split_axis=0, concat_axis=0, tiled=True)
    out = pl.pallas_call(
        functools.partial(unpack, members, rows),
        out_shape=jax.ShapeDtypeStruct((members * 2 * rows, LANES), F32),
        in_specs=[VMEM],
        out_specs=HBM,
        scratch_shapes=[
            pltpu.VMEM((members * 2 * rows, LANES), F32),
            pltpu.SemaphoreType.DMA((PIECES,)),
        ],
        compiler_params=pltpu.CompilerParams(vmem_limit_bytes=16 << 20),
        name="unpack",
    )(in_vmem(returned))
    return out.reshape(members, 2, rows, LANES).transpose(0, 2, 1, 3).reshape(members, rows, lon)


def solution(mesh):
    return jax.shard_map(
        shards,
        mesh=mesh,
        in_specs=(
            P("mem", "band", None),
            P(None, "band", None),
            P("band", None, None),
            P("band", None),
            P(),
            P("band", None),
        ),
        out_specs=P("mem", "band", None),
        check_vma=False,
    )
```
